256 devices in a mesh: member: 8 (over y, z_hi), tile: 32 (over z_lo, x, core).
Axes of the slice: x: 4, y: 4, z: 8 (z_hi: 2, z_lo: 4; z = z_hi * 4 + z_lo), core: 2. Of those that a mesh axis runs over, the one named last changes fastest.
Arguments:
- surface: float32 [16, 1024, 512], P('member', 'tile'), may hold values from -6 to 6
- depth: float32 [1024, 512], P('tile'), may hold values from 0.32 to 0.45
- land: int32 [1024, 512], P('tile'), may hold values from 0 to 1, as said below
- gauge_cells: int32 [400], replicated, may hold values from 0 to 524287, as said below
- sigma: float32 [400], replicated, may hold values from 0.2 to 1
- observed: float32 [9600], replicated, may hold values from -4 to 4
- noise: float32 [16, 9600], P('member'), may hold values from -3 to 3
Outputs:
- updated: float32 [16, 1024, 512], P('member', 'tile')
- records: float32 [16, 9600], P('member', 'tile')
The draws below stay inside these ranges and needn't reach their ends.
Inputs may be any that keep to these rules, and one draw needn't show every extreme that they name: `gauge_cells`: every block of 32 rows starting at a multiple of 32 holds a gauge in its first row and one in its last row. `land`: every gauge cell and the cells directly above and below it (rows taken periodically) are sea.
All inputs are finite; a program needn't handle non-finite values.
Results may differ from the reference program's by a relative error of at most 0.00022.
Values sent between devices are 32-bit elements; how exact they have to be, the bound alone decides.
A program may use at most 64 MiB of HBM per device.

```python
import math
import jax
import jax.numpy as jnp
from jax import lax

CX = 32
NY = 512
STEPS = 24
GAUGES = 400
MEMBERS = 16
NX = 1024
DATA = 9600


def gauge_layout(key):
    strip_total = NX // CX
    index = jnp.arange(GAUGES, dtype=jnp.int32)
    strip = index % strip_total
    layer = index // strip_total
    random_rows = jax.random.randint(jax.random.fold_in(key, 11), (GAUGES,), 0, CX, dtype=jnp.int32)
    offset = jnp.where(layer == 0, CX - 1, jnp.where(layer == 1, 0, random_rows))
    columns = jax.random.randint(jax.random.fold_in(key, 12), (GAUGES,), 0, NY, dtype=jnp.int32)
    cells = (strip * CX + offset) * NY + columns
    cells = cells.at[strip_total - 1].set(NX * NY - 1)
    cells = cells.at[strip_total].set(0)
    return cells.astype(jnp.int32)


def draw_gauge_cells(key, part):
    return gauge_layout(key)


def draw_land(key, part):
    cells = gauge_layout(key)
    total = NX * NY
    coarse = jax.random.randint(jax.random.fold_in(key, 13), (total,), 0, 32, dtype=jnp.int32)
    flat = jnp.where(coarse != 0, 1, 0).astype(jnp.int32)
    flat = flat.at[cells].set(1)
    flat = flat.at[(cells + NY) % total].set(1)
    flat = flat.at[(cells + total - NY) % total].set(1)
    return flat.reshape(NX, NY)


def draw_depth(key, part):
    values = jax.random.uniform(jax.random.fold_in(key, 22), (NX, NY), jnp.float32, 0.32, 0.45)
    return values.astype(jnp.float32)


def block_levels(stream_key, extent, pieces, low, largest):
    gain, own = 1.0, jax.random.fold_in(stream_key, 6)
    for dim, shards_of in pieces:
        heights = jnp.exp(jax.random.uniform(jax.random.fold_in(own, dim), (shards_of,), jnp.float32, low / len(pieces), largest / len(pieces)))
        gain = gain * jnp.repeat(heights, extent[dim] // shards_of).reshape([-1 if axis == dim else 1 for axis in range(len(extent))])
    return gain


def normal_values(key, dims, scale, reach, pieces=(), kind=jnp.bfloat16):
    entries = scale * jax.random.normal(key, dims, jnp.float32)
    if pieces:
        entries = entries * block_levels(key, dims, pieces, -0.22, 0.18)
    return jnp.clip(entries, -reach, reach).astype(kind)


def setup_inputs(seed: int = 0) -> dict:
    keys = jax.random.split(jax.random.key(seed), 8)
    surface = normal_values(keys[0], (MEMBERS, NX, NY), 1.0, 6.0, ((0, 8), (1, 32)), jnp.float32)
    depth = draw_depth(jax.random.fold_in(keys[7], 71), 0)
    land = draw_land(jax.random.fold_in(keys[7], 71), 0)
    gauge_cells = draw_gauge_cells(jax.random.fold_in(keys[7], 71), 0)
    sigma = jnp.clip(jnp.exp(jax.random.uniform(keys[4], (GAUGES,), jnp.float32, math.log(0.2), math.log(1.0))), 0.2, 1.0)
    observed = normal_values(keys[5], (DATA,), 0.5, 4.0, (), jnp.float32)
    noise = normal_values(keys[6], (MEMBERS, DATA), 0.3, 3.0, ((0, 8),), jnp.float32)
    return {"surface": surface, "depth": depth, "land": land, "gauge_cells": gauge_cells, "sigma": sigma, "observed": observed, "noise": noise}


def chol_solve(factor, rhs):
    middle = lax.linalg.triangular_solve(factor, rhs, left_side=True, lower=True, transpose_a=False)
    return lax.linalg.triangular_solve(factor, middle, left_side=True, lower=True, transpose_a=True)

def evolve(surface, depth, land, gauge_cells):
    wet_depth = depth * land.astype(jnp.float32)
    zero_col = jnp.zeros((wet_depth.shape[0], 1), jnp.float32)
    coeff_rows = jnp.minimum(wet_depth, jnp.roll(wet_depth, -1, 0))
    coeff_cols = jnp.minimum(wet_depth, jnp.concatenate([wet_depth[:, 1:], zero_col], 1))
    member_count = surface.shape[0]
    level_col = jnp.zeros((member_count, surface.shape[1], 1), jnp.float32)

    def advance(carry, ignored):
        level, flux_rows, flux_cols = carry
        below = jnp.roll(level, -1, 1)
        flux_rows = flux_rows - coeff_rows * (below - level)
        beside = jnp.concatenate([level[:, :, 1:], level_col], 2)
        flux_cols = flux_cols - coeff_cols * (beside - level)
        above = jnp.roll(flux_rows, 1, 1)
        left = jnp.concatenate([level_col, flux_cols[:, :, :-1]], 2)
        level = level - (flux_rows - above + flux_cols - left)
        sample = jnp.take(level.reshape(member_count, -1), gauge_cells, axis=1)
        return ((level, flux_rows, flux_cols), sample)
    start = (surface, jnp.zeros_like(surface), jnp.zeros_like(surface))
    final, samples = lax.scan(advance, start, None, length=STEPS)
    return jnp.transpose(samples, (1, 0, 2)).reshape(member_count, -1)

def reference(surface, depth, land, gauge_cells, sigma, observed, noise):
    records = evolve(surface, depth, land, gauge_cells)
    innovation = observed[None, :] + noise - records
    weight = jnp.tile(1.0 / (sigma * sigma), STEPS)
    anomaly = records - jnp.mean(records, axis=0, keepdims=True)
    gram_ss = jnp.dot(anomaly * weight[None, :], anomaly.T, precision=lax.Precision.HIGHEST)
    gram_se = jnp.dot(anomaly * weight[None, :], innovation.T, precision=lax.Precision.HIGHEST)
    identity = jnp.eye(MEMBERS, dtype=jnp.float32)
    system = gram_ss + (MEMBERS - 1.0) * identity
    factor = jnp.linalg.cholesky(system)
    mixing = chol_solve(factor, gram_se)
    combine = identity + mixing - jnp.mean(mixing, axis=0, keepdims=True)
    updated = jnp.einsum('kxy,km->mxy', surface, combine, precision=lax.Precision.HIGHEST)
    return (updated, records)
```

```python
import functools

import jax
import jax.numpy as jnp
from jax import lax
from jax.experimental import pallas as pl
from jax.experimental.pallas import tpu as pltpu
from jax.sharding import PartitionSpec as P

MESH = pl.DeviceIdType.MESH
STEPS = 24
HALO = 24
OWN = 32
ROWS = 96
COLT = 4
PLANE = 8
PLANES = 4
MEMBER_DEV = 8


def remote(src, dst, send, recv, member=None, tile=None):
    device = {}
    if member is not None:
        device["member"] = member
    if tile is not None:
        device["tile"] = tile
    return pltpu.make_async_remote_copy(
        src_ref=src, dst_ref=dst, send_sem=send, recv_sem=recv, device_id=device, device_id_type=MESH
    )


def next_col(value, lane, axis):
    rolled = pltpu.roll(value, 127, value.ndim - 1)
    first = lax.slice_in_dim(rolled, 0, 1, axis=axis)
    rest = lax.slice_in_dim(rolled, 1, COLT, axis=axis)
    return jnp.where(lane == 127, jnp.concatenate([rest, first], axis), rolled)


def prev_col(value, lane, axis):
    rolled = pltpu.roll(value, 1, value.ndim - 1)
    last = lax.slice_in_dim(rolled, COLT - 1, COLT, axis=axis)
    rest = lax.slice_in_dim(rolled, 0, COLT - 1, axis=axis)
    return jnp.where(lane == 0, jnp.concatenate([last, rest], axis), rolled)


def window(ref, start, lane):
    tiles = ref.shape[1] // 128
    tile = start // 128
    shift = start % 128
    after = jnp.minimum(tile + 1, tiles - 1)
    low = ref[:, pl.ds(pl.multiple_of(tile * 128, 128), 128)]
    high = ref[:, pl.ds(pl.multiple_of(after * 128, 128), 128)]
    both = jnp.where(lane < 128 - shift, pltpu.roll(low, 128 - shift, 1), pltpu.roll(high, 128 - shift, 1))
    return jnp.where(lane < 100, both, 0.0)


def kernel(
    surface, depth, land, cells, sigma, observed, noise, updated, records,
    state, frow, fcol, crow, ccol, hist, every, pieces, got1, mine, got2, own_noise, all_noise, obs, weight,
    plane_got, gram, gram1, gram_plane, gram2, coef,
    local_sem, halo_send, halo_recv, noise_send, noise_recv, s1_send, s1_recv, s2_send, s2_recv,
    zl_send, zl_recv, g1_send, g1_recv, g2_send, g2_recv, sur_send, sur_recv,
):
    a = lax.axis_index("member")
    t = lax.axis_index("tile")
    z = t // PLANE
    c = t % PLANE
    y = a // 2
    hi = a % 2
    tiles = PLANE * PLANES
    partner = a + 1 - 2 * hi
    y_next = ((y + 1) % 4) * 2
    y_prev = ((y + 3) % 4) * 2

    barrier = pltpu.get_barrier_semaphore()

    def greet(**device):
        pl.semaphore_signal(barrier, inc=1, device_id=device, device_id_type=MESH)

    for k in range(1, MEMBER_DEV):
        greet(member=(a + k) % MEMBER_DEV)
    for k in range(1, PLANE):
        greet(tile=z * PLANE + (c + k) % PLANE)
    for k in range(1, PLANES):
        greet(tile=((z + k) % PLANES) * PLANE + c)
    greet(tile=(t + 1) % tiles)
    greet(tile=(t + tiles - 1) % tiles)

    loads = [
        pltpu.make_async_copy(
            surface.at[:, :, pl.ds(i * 128, 128)], state.at[pl.ds(0, 2), i, pl.ds(OWN, 32), :], local_sem.at[i]
        )
        for i in range(COLT)
    ]
    for load in loads:
        load.start()
    keep = pltpu.make_async_copy(surface, every.at[a], local_sem.at[COLT])
    keep.start()

    for i in range(COLT):
        columns = slice(i * 128, (i + 1) * 128)
        state[2, i, OWN:OWN + 32, :] = depth[:, columns] * land[:, columns].astype(jnp.float32)
    state[:, :, 0:8, :] = jnp.zeros((3, COLT, 8, 128), jnp.float32)
    state[:, :, ROWS - 8:ROWS, :] = jnp.zeros((3, COLT, 8, 128), jnp.float32)
    for r in range(0, ROWS, 8):
        frow[:, :, r:r + 8, :] = jnp.zeros((2, COLT, 8, 128), jnp.float32)
        fcol[:, :, r:r + 8, :] = jnp.zeros((2, COLT, 8, 128), jnp.float32)
    for load in loads:
        load.wait()
    pl.semaphore_wait(barrier, MEMBER_DEV - 1 + PLANE - 1 + PLANES - 1 + 2)

    up = remote(
        state.at[:, :, pl.ds(OWN, HALO), :], state.at[:, :, pl.ds(OWN + 32, HALO), :],
        halo_send.at[0], halo_recv.at[0], tile=(t + tiles - 1) % tiles,
    )
    down = remote(
        state.at[:, :, pl.ds(OWN + 32 - HALO, HALO), :], state.at[:, :, pl.ds(OWN - HALO, HALO), :],
        halo_send.at[1], halo_recv.at[1], tile=(t + 1) % tiles,
    )
    up.start()
    down.start()

    def block(number, slot, member, part=None):
        ref = every.at[slot] if part is None else every.at[slot, part]
        return remote(ref, ref, sur_send.at[number], sur_recv.at[number], member=member)

    keep.wait()
    to_partner = block(0, a, partner)
    to_next = block(1, a, y_next + hi)
    to_prev = block(2, a, y_prev + hi)
    to_partner.start()
    to_next.start()
    to_prev.start()

    lane1 = lax.broadcasted_iota(jnp.int32, (1, 128), 1)
    lane2 = lax.broadcasted_iota(jnp.int32, (2, 128), 1)
    for p in range(PLANES):
        own_noise[p, 6:8, :] = jnp.zeros((2, 128), jnp.float32)
        for r in range(3):
            unit = (p * PLANE + c) * 3 + r
            own_noise[p, 2 * r:2 * r + 2, :] = window(noise, unit * 100, lane2)
            obs[p, r:r + 1, :] = window(observed, unit * 100, lane1)
    for q in range(4):
        weight[q:q + 1, :] = sigma[q:q + 1, :]
    all_noise[a] = own_noise[...]
    noise_copies = []
    for k in range(1, MEMBER_DEV):
        noise_copies.append(
            remote(own_noise, all_noise.at[a], noise_send.at[k], noise_recv.at[a], member=(a + k) % MEMBER_DEV)
        )
        noise_copies[-1].start()

    up.wait()
    down.wait()

    lane3 = lax.broadcasted_iota(jnp.int32, (COLT, 8, 128), 2)
    tile3 = lax.broadcasted_iota(jnp.int32, (COLT, 8, 128), 0)
    for r in range(8, ROWS - 8, 8):
        wet = state[2, :, r:r + 8, :]
        crow[:, r:r + 8, :] = jnp.minimum(wet, state[2, :, r + 1:r + 9, :])
        beside = jnp.where((lane3 == 127) & (tile3 == COLT - 1), 0.0, next_col(wet, lane3, 0))
        ccol[:, r:r + 8, :] = jnp.minimum(wet, beside)

    lane4 = lax.broadcasted_iota(jnp.int32, (2, COLT, 8, 128), 3)

    def advance(first, last, s):
        for b in range(first, last):
            r = 8 + 8 * b
            level = state[0:2, :, r:r + 8, :]
            below = state[0:2, :, r + 1:r + 9, :]
            rows_flux = frow[:, :, r:r + 8, :] - crow[:, r:r + 8, :][None] * (below - level)
            frow[:, :, r:r + 8, :] = rows_flux
            beside = next_col(level, lane4, 1)
            cols_flux = fcol[:, :, r:r + 8, :] - ccol[:, r:r + 8, :][None] * (beside - level)
            fcol[:, :, r:r + 8, :] = cols_flux
            above = frow[:, :, r - 1:r + 7, :]
            left = prev_col(cols_flux, lane4, 1)
            level = level - (rows_flux - above + cols_flux - left)
            state[0:2, :, r:r + 8, :] = level
            if 3 <= b < 7:
                for m in range(2):
                    for i in range(COLT):
                        hist[pl.ds(i * 32 + 8 * (b - 3), 8), 2 * s + m, :] = level[m, i]

    for phase in range(3):
        def one(s, carry, phase=phase):
            advance(phase, 10 - phase, s)
            return carry

        lax.fori_loop(8 * phase, 8 * phase + 8, one, 0)

    lane48 = lax.broadcasted_iota(jnp.int32, (2 * STEPS, 128), 1)
    base = t * (32 * 512)

    def sample(j, totals):
        out = []
        for q in range(4):
            local = cells[q * 100 + j] - base
            here = (local >= 0) & (local < 32 * 512)
            cell = jnp.clip(local, 0, 32 * 512 - 1)
            col = cell % 512
            found = hist[(col // 128) * 32 + cell // 512]
            moved = pltpu.roll(found, (j - col % 128 + 128) % 128, 1)
            lane_here = jnp.where(here, j, -1)
            out.append(jnp.where(lane48 == lane_here, moved, totals[q]))
        return tuple(out)

    zero48 = jnp.zeros((2 * STEPS, 128), jnp.float32)
    totals = lax.fori_loop(0, 100, sample, (zero48,) * 4)
    for p in range(PLANES):
        for k in range(PLANE):
            pieces[k, p, 6:8, :] = jnp.zeros((2, 128), jnp.float32)
            for r in range(3):
                unit = (p * PLANE + k) * 3 + r
                s, q = unit // 4, unit % 4
                pieces[k, p, 2 * r:2 * r + 2, :] = totals[q][2 * s:2 * s + 2, :]

    copies1 = []
    for k in range(1, PLANE):
        other = (c + k) % PLANE
        copies1.append(
            remote(pieces.at[other], got1.at[c], s1_send.at[k], s1_recv.at[c], tile=z * PLANE + other)
        )
        copies1[-1].start()
    total = pieces[c]
    for k in range(1, PLANE):
        other = (c + k) % PLANE
        remote(pieces.at[other], got1.at[other], s1_send.at[k], s1_recv.at[other], tile=z * PLANE + other).wait_recv()
        total = total + got1[other]
    mine[...] = total
    got2[a] = total

    copies2 = []
    for k in range(1, MEMBER_DEV):
        other = (a + k) % MEMBER_DEV
        copies2.append(remote(mine, got2.at[a], s2_send.at[k], s2_recv.at[a], member=other))
        copies2[-1].start()
    copies_z = []
    for k in range(1, PLANES):
        other = (z + k) % PLANES
        copies_z.append(
            remote(mine.at[other], plane_got.at[z], zl_send.at[k], zl_recv.at[z], tile=other * PLANE + c)
        )
        copies_z[-1].start()

    to_next.wait()
    to_prev.wait()
    on_next = block(3, y_prev + hi, y_next + hi, 0)
    on_prev = block(4, y_next + hi, y_prev + hi, 1)
    on_next.start()
    on_prev.start()

    for k in range(1, MEMBER_DEV):
        other = (a + k) % MEMBER_DEV
        remote(own_noise, all_noise.at[other], noise_send.at[k], noise_recv.at[other], member=other).wait_recv()
    for k in range(1, MEMBER_DEV):
        other = (a + k) % MEMBER_DEV
        remote(mine, got2.at[other], s2_send.at[k], s2_recv.at[other], member=other).wait_recv()

    lefts, rights = [], []
    for p in range(PLANES):
        for r in range(3):
            group = ((p * PLANE + c) * 3 + r) % 4
            sig = weight[pl.ds(group, 1), :]
            wgt = jnp.where(lane1 < 100, 1.0 / (sig * sig), 0.0)
            rec = got2[:, p, 2 * r:2 * r + 2, :].reshape(16, 128)
            nse = all_noise[:, p, 2 * r:2 * r + 2, :].reshape(16, 128)
            innovation = obs[p, r:r + 1, :] + nse - rec
            anomaly = rec - jnp.sum(rec, axis=0, keepdims=True) * (1.0 / 16.0)
            lefts.append(anomaly * wgt)
            rights.append(jnp.concatenate([anomaly, innovation], 0))
    left = jnp.concatenate(lefts, 1)
    right = jnp.concatenate(rights, 1)
    both = lax.dot_general(
        left, right, (((1,), (1,)), ((), ())), precision=lax.Precision.HIGHEST, preferred_element_type=jnp.float32
    )
    gram[:, 0:32] = both

    def exchange(count, me, src, dst, send, recv, tile_of):
        sent = []
        for k in range(1, count):
            other = (me + k) % count
            sent.append(remote(src, dst.at[me], send.at[k], recv.at[me], tile=tile_of(other)))
            sent[-1].start()
        return sent

    def collect(count, me, src, dst, send, recv, tile_of):
        total = None
        for k in range(1, count):
            other = (me + k) % count
            remote(src, dst.at[other], send.at[k], recv.at[other], tile=tile_of(other)).wait_recv()
        for k in range(count):
            total = dst[k] if total is None else total + dst[k]
        return total

    def in_plane(other):
        return z * PLANE + other

    def across(other):
        return other * PLANE + c

    gram1[c] = gram[...]
    sent1 = exchange(PLANE, c, gram, gram1, g1_send, g1_recv, in_plane)

    to_partner.wait()
    par_next = block(5, partner, y_next + hi)
    par_prev = block(6, partner, y_prev + hi)
    par_next.start()
    par_prev.start()

    plane_total = collect(PLANE, c, gram, gram1, g1_send, g1_recv, in_plane)
    gram_plane[...] = plane_total
    gram2[z] = plane_total
    sent2 = exchange(PLANES, z, gram_plane, gram2, g2_send, g2_recv, across)

    block_rows = mine[z]
    for k in range(1, PLANES):
        other = (z + k) % PLANES
        remote(mine.at[other], plane_got.at[other], zl_send.at[k], zl_recv.at[other], tile=other * PLANE + c).wait_recv()
        block_rows = block_rows + plane_got[other]
    for r in range(3):
        records[:, 100 * r:100 * r + 100] = block_rows[2 * r:2 * r + 2, 0:100]

    par_next.wait()
    par_prev.wait()
    last_next = block(7, y_prev + 1 - hi, y_next + hi, 0)
    last_prev = block(8, y_next + 1 - hi, y_prev + hi, 1)
    last_next.start()
    last_prev.start()

    system = collect(PLANES, z, gram_plane, gram2, g2_send, g2_recv, across)

    lane16 = lax.broadcasted_iota(jnp.int32, (16, 128), 1)
    row16 = lax.broadcasted_iota(jnp.int32, (16, 128), 0)
    system = jnp.where(lane16 < 32, system, 0.0) + jnp.where(row16 == lane16, 15.0, 0.0)
    for p in range(16):
        pivot = system[p:p + 1, :] / system[p:p + 1, p:p + 1]
        system = jnp.where(row16 == p, pivot, system - system[:, p:p + 1] * pivot)
    combine = system - jnp.sum(system, axis=0, keepdims=True) * (1.0 / 16.0)
    combine = combine + jnp.where(row16 == lane16 - 16, 1.0, 0.0)
    for m in range(2):
        column = jnp.sum(jnp.where(lane16 == 16 + 2 * a + m, combine, 0.0), axis=1, keepdims=True)
        coef[m] = jnp.broadcast_to(column, (16, 128))

    on_next.wait()
    on_prev.wait()
    last_next.wait()
    last_prev.wait()

    factors = [[jnp.broadcast_to(coef[m, k:k + 1, :], (8, 128)) for k in range(16)] for m in range(2)]
    for r in range(0, 32, 8):
        for i in range(COLT):
            columns = slice(i * 128, (i + 1) * 128)
            sums = [None, None]
            for k in range(16):
                value = every[k // 2, k % 2, r:r + 8, columns]
                for m in range(2):
                    term = value * factors[m][k]
                    sums[m] = term if sums[m] is None else sums[m] + term
            for m in range(2):
                updated[m, r:r + 8, columns] = sums[m]

    for copy in noise_copies + copies1 + copies2 + copies_z + sent1 + sent2:
        copy.wait_send()


def shards(surface, depth, land, gauge_cells, sigma, observed, noise):
    f32 = jnp.float32
    groups = jnp.pad(sigma.reshape(4, 100), ((0, 0), (0, 28)), constant_values=1.0)
    vmem = pl.BlockSpec(memory_space=pltpu.VMEM)
    dma = pltpu.SemaphoreType.DMA
    return pl.pallas_call(
        kernel,
        out_shape=(jax.ShapeDtypeStruct((2, 32, 512), f32), jax.ShapeDtypeStruct((2, 300), f32)),
        in_specs=[
            pl.BlockSpec(memory_space=pl.ANY), vmem, vmem, pl.BlockSpec(memory_space=pltpu.SMEM), vmem, vmem, vmem,
        ],
        out_specs=(vmem, vmem),
        scratch_shapes=[
            pltpu.VMEM((3, COLT, ROWS, 128), f32),
            pltpu.VMEM((2, COLT, ROWS, 128), f32),
            pltpu.VMEM((2, COLT, ROWS, 128), f32),
            pltpu.VMEM((COLT, ROWS, 128), f32),
            pltpu.VMEM((COLT, ROWS, 128), f32),
            pltpu.VMEM((128, 2 * STEPS, 128), f32),
            pltpu.VMEM((MEMBER_DEV, 2, 32, 512), f32),
            pltpu.VMEM((PLANE, PLANES, 8, 128), f32),
            pltpu.VMEM((PLANE, PLANES, 8, 128), f32),
            pltpu.VMEM((PLANES, 8, 128), f32),
            pltpu.VMEM((MEMBER_DEV, PLANES, 8, 128), f32),
            pltpu.VMEM((PLANES, 8, 128), f32),
            pltpu.VMEM((MEMBER_DEV, PLANES, 8, 128), f32),
            pltpu.VMEM((PLANES, 8, 128), f32),
            pltpu.VMEM((8, 128), f32),
            pltpu.VMEM((PLANES, 8, 128), f32),
            pltpu.VMEM((16, 128), f32),
            pltpu.VMEM((PLANE, 16, 128), f32),
            pltpu.VMEM((16, 128), f32),
            pltpu.VMEM((PLANES, 16, 128), f32),
            pltpu.VMEM((2, 16, 128), f32),
            dma((5,)),
            dma((2,)), dma((2,)),
            dma((8,)), dma((8,)),
            dma((8,)), dma((8,)),
            dma((8,)), dma((8,)),
            dma((4,)), dma((4,)),
            dma((8,)), dma((8,)),
            dma((4,)), dma((4,)),
            dma((9,)), dma((9,)),
        ],
        compiler_params=pltpu.CompilerParams(collective_id=0, has_side_effects=True),
    )(surface, depth, land, gauge_cells, groups, observed.reshape(1, -1), noise)


def solution(mesh):
    in_specs = (
        P("member", "tile", None),
        P("tile", None),
        P("tile", None),
        P(),
        P(),
        P(),
        P("member", None),
    )
    out_specs = (P("member", "tile", None), P("member", "tile"))
    return jax.shard_map(shards, mesh=mesh, in_specs=in_specs, out_specs=out_specs, check_vma=False)
```

```python
import jax
import jax.numpy as jnp
from jax import lax
from jax.experimental import pallas as pl
from jax.experimental.pallas import tpu as pltpu
from jax.sharding import PartitionSpec as P

MESH = pl.DeviceIdType.MESH
HALO = 24
OWN = 32
ROWS = OWN + 2 * HALO
PLANE = 8
PLANES = 4
MEMBER_DEV = 8
NO_GAUGE = OWN * 32


def remote(src, dst, send, recv, **device):
    return pltpu.make_async_remote_copy(
        src_ref=src, dst_ref=dst, send_sem=send, recv_sem=recv, device_id=device, device_id_type=MESH
    )


def next_col(value, lane):
    rolled = pltpu.roll(value, 127, value.ndim - 1)
    return jnp.where(lane == 127, pltpu.roll(rolled, 7, value.ndim - 2), rolled)


def prev_col(value, lane):
    rolled = pltpu.roll(value, 1, value.ndim - 1)
    return jnp.where(lane == 0, pltpu.roll(rolled, 1, value.ndim - 2), rolled)


def merge(low, high, shift, lane):
    both = jnp.where(lane < 128 - shift, pltpu.roll(low, 128 - shift, 1), pltpu.roll(high, 128 - shift, 1))
    return jnp.where(lane < 100, both, 0.0)


def kernel(
    surface, depth, land, cells_in, sigma_in, observed_in, noise_in, updated, records,
    depth_v, land_v, cells, sigma, observed, noise, starts, shifts,
    lev, wet, frow, fcol, crow, ccol, hist, every, pieces, got1, mine, got2, own_noise, all_noise, obs,
    plane_got, block_rows, gram, gram1, gram_plane, gram2, coef,
    local_sem, halo_send, halo_recv, noise_send, noise_recv, s1_send, s1_recv, s2_send, s2_recv,
    zl_send, zl_recv, g1_send, g1_recv, g2_send, g2_recv, sur_send, sur_recv,
):
    a = lax.axis_index("member")
    t = lax.axis_index("tile")
    z = t // PLANE
    c = t % PLANE
    y = a // 2
    hi = a % 2
    tiles = PLANE * PLANES
    partner = a + 1 - 2 * hi
    y_next = ((y + 1) % 4) * 2
    y_prev = ((y + 3) % 4) * 2
    above_tile = (t + tiles - 1) % tiles
    below_tile = (t + 1) % tiles

    barrier = pltpu.get_barrier_semaphore()

    def greet(**device):
        pl.semaphore_signal(barrier, inc=1, device_id=device, device_id_type=MESH)

    for k in range(1, MEMBER_DEV):
        greet(member=(a + k) % MEMBER_DEV)
    greet(tile=below_tile)
    greet(tile=above_tile)
    for k in range(1, PLANES):
        greet(tile=((z + k) % PLANES) * PLANE + c)
    for k in range(1, PLANE):
        greet(tile=z * PLANE + (c + k) % PLANE)

    def local(number, src, dst):
        copy = pltpu.make_async_copy(src, dst, local_sem.at[number])
        copy.start()
        return copy

    loads = [local(0, depth, depth_v), local(1, land, land_v)]
    loads += [
        local(
            2 + 4 * m + i,
            surface.at[m, :, pl.ds(i * 128, 128)],
            lev.at[pl.ds(HALO, OWN), 4 * m + i, :],
        )
        for m in range(2)
        for i in range(4)
    ]
    keep = local(10, surface, every.at[a])
    late = [local(11, noise_in, noise), local(12, observed_in, observed), local(13, sigma_in, sigma)]
    table = local(14, cells_in, cells)

    lane = lax.broadcasted_iota(jnp.int32, (8, 128), 1)
    sub = lax.broadcasted_iota(jnp.int32, (8, 128), 0)
    zero = jnp.zeros((8, 128), jnp.float32)
    for r in range(ROWS):
        frow[r] = zero
        fcol[r] = zero
    for s in range(6):
        for p in range(4):
            hist[pl.ds(((s * (OWN + 1) + OWN) * 4 + p) * 8, 8), :] = zero
    loads[0].wait()
    loads[1].wait()
    for r in range(0, OWN, 8):
        for i in range(4):
            columns = slice(i * 128, (i + 1) * 128)
            value = depth_v[r:r + 8, columns] * land_v[r:r + 8, columns].astype(jnp.float32)
            wet[pl.ds((HALO + r) * 4 + i, 8, stride=4), :] = value
    for load in loads[2:]:
        load.wait()
    pl.semaphore_wait(barrier, MEMBER_DEV - 1 + PLANE - 1 + PLANES - 1 + 2)

    halos = [
        remote(lev.at[pl.ds(HALO, HALO)], lev.at[pl.ds(HALO + OWN, HALO)], halo_send.at[0], halo_recv.at[0], tile=above_tile),
        remote(lev.at[pl.ds(OWN, HALO)], lev.at[pl.ds(0, HALO)], halo_send.at[1], halo_recv.at[1], tile=below_tile),
        remote(
            wet.at[pl.ds(HALO * 4, HALO * 4)], wet.at[pl.ds((HALO + OWN) * 4, HALO * 4)],
            halo_send.at[2], halo_recv.at[2], tile=above_tile,
        ),
        remote(
            wet.at[pl.ds(OWN * 4, HALO * 4)], wet.at[pl.ds(0, HALO * 4)],
            halo_send.at[3], halo_recv.at[3], tile=below_tile,
        ),
    ]
    for copy in halos:
        copy.start()

    def block(number, slot, member, part=None):
        ref = every.at[slot] if part is None else every.at[slot, part]
        return remote(ref, ref, sur_send.at[number], sur_recv.at[number], member=member)

    keep.wait()
    to_partner = block(0, a, partner)
    to_next = block(1, a, y_next + hi)
    to_prev = block(2, a, y_prev + hi)
    to_partner.start()
    to_next.start()
    to_prev.start()

    lane1 = lax.broadcasted_iota(jnp.int32, (1, 128), 1)
    lane2 = lax.broadcasted_iota(jnp.int32, (2, 128), 1)
    for load in late:
        load.wait()
    for p in range(PLANES):
        for r in range(3):
            start = ((p * PLANE + c) * 3 + r) * 100
            first, shift = start // 128, start % 128
            after = jnp.minimum(first + 1, 74)
            own_noise[r, 2 * p:2 * p + 2, :] = merge(
                noise[:, pl.ds(pl.multiple_of(first * 128, 128), 128)],
                noise[:, pl.ds(pl.multiple_of(after * 128, 128), 128)],
                shift, lane2,
            )
            obs[r, p:p + 1, :] = merge(observed[pl.ds(first, 1), :], observed[pl.ds(after, 1), :], shift, lane1)
    all_noise[a] = own_noise[...]
    noise_copies = []
    for k in range(1, MEMBER_DEV):
        noise_copies.append(
            remote(own_noise, all_noise.at[a], noise_send.at[k], noise_recv.at[a], member=(a + k) % MEMBER_DEV)
        )
        noise_copies[-1].start()

    table.wait()

    def entry(j, carry):
        for q in range(4):
            cell = cells[q * 100 + j]
            start = ((cell >> 9) & 31) * 32 + ((cell >> 7) & 3)
            starts[q * 100 + j] = jnp.where((cell >> 14) == t, start, NO_GAUGE)
            shifts[q * 100 + j] = (j - cell) & 127
        return carry

    lax.fori_loop(0, 100, entry, 0, unroll=5)

    edge = (lane == 127) & ((sub & 3) == 3)

    def both_rows(pair):
        value = wet[8 * pair:8 * pair + 8, :]
        other = pltpu.roll(value, 4, 0)
        return [jnp.where(sub < 4, value, other), jnp.where(sub < 4, other, value)]

    def coefficients(first, last):
        below = None
        for pair in range(last // 2 - 1, first // 2 - 1, -1):
            even, odd = both_rows(pair)
            if below is None:
                below = both_rows(last // 2)[0] if last < ROWS else zero
            for r, value, following in ((2 * pair + 1, odd, below), (2 * pair, even, odd)):
                crow[r] = jnp.minimum(value, following)
                ccol[r] = jnp.minimum(value, jnp.where(edge, 0.0, next_col(value, lane)))
            below = even

    coefficients(HALO, HALO + OWN - 2)
    for copy in halos:
        copy.wait()
    coefficients(0, HALO)
    coefficients(HALO + OWN - 2, ROWS)

    def advance(first, s):
        low, high = first + 1, ROWS - 1 - first
        level = lev[low - 1:low]
        flux = frow[low - 1:low] - crow[low - 1:low] * (lev[low:low + 1] - level)
        frow[low - 1:low] = flux
        group = (s % 6) * (OWN + 1)
        for start in range(low, high, 8):
            stop = min(start + 8, high)
            lane3 = lax.broadcasted_iota(jnp.int32, (stop - start, 8, 128), 2)
            level = lev[start:stop]
            rows_flux = frow[start:stop] - crow[start:stop] * (lev[start + 1:stop + 1] - level)
            frow[start:stop] = rows_flux
            cols_flux = fcol[start:stop] - ccol[start:stop] * (next_col(level, lane3) - level)
            fcol[start:stop] = cols_flux
            above = jnp.concatenate([flux, rows_flux[:-1]], 0)
            flux = rows_flux[-1:]
            level = level - (rows_flux - above + cols_flux - prev_col(cols_flux, lane3))
            lev[start:stop] = level
            for r in range(max(start, HALO), min(stop, HALO + OWN)):
                flat = ((group + (r - HALO)) * 4 + s // 6) * 8
                hist[pl.ds(pl.multiple_of(flat, 8), 8), :] = level[r - start]

    for first in range(0, 24, 8):
        def one(s, carry, first=first):
            advance(first, s)
            return carry

        lax.fori_loop(first, first + 8, one, 0)

    def sample(j, totals):
        put = lane == j
        out = []
        for q in range(4):
            start = starts[q * 100 + j]
            shift = shifts[q * 100 + j]
            for s in range(6):
                found = hist[pl.ds(s * (OWN + 1) * 32 + start, 8, stride=4), :]
                out.append(jnp.where(put, pltpu.roll(found, shift, 1), totals[q * 6 + s]))
        return tuple(out)

    totals = lax.fori_loop(0, 100, sample, (zero,) * 24, unroll=4)
    for q in range(4):
        for s in range(6):
            pieces[4 * s + q] = totals[q * 6 + s]

    copies1 = []
    for k in range(1, PLANE):
        other = (c + k) % PLANE
        copies1.append(
            remote(pieces.at[pl.ds(other * 3, 3)], got1.at[c], s1_send.at[k], s1_recv.at[c], tile=z * PLANE + other)
        )
        copies1[-1].start()
    total = pieces[pl.ds(c * 3, 3)]
    for k in range(1, PLANE):
        other = (c + k) % PLANE
        remote(
            pieces.at[pl.ds(other * 3, 3)], got1.at[other], s1_send.at[k], s1_recv.at[other], tile=z * PLANE + other
        ).wait_recv()
        total = total + got1[other]
    mine[...] = total
    for r in range(3):
        got2[pl.ds(pl.multiple_of(a * 24 + 8 * r, 8), 8), :] = total[r]

    def slot(ref, number):
        return ref.at[pl.ds(pl.multiple_of(number * 24, 8), 24)]

    flat_mine = got2.at[pl.ds(pl.multiple_of(a * 24, 8), 24)]
    copies2 = []
    for k in range(1, MEMBER_DEV):
        other = (a + k) % MEMBER_DEV
        copies2.append(remote(flat_mine, slot(got2, a), s2_send.at[k], s2_recv.at[a], member=other))
        copies2[-1].start()
    copies_z = []
    for k in range(1, PLANES):
        other = (z + k) % PLANES
        copies_z.append(remote(mine, plane_got.at[z], zl_send.at[k], zl_recv.at[z], tile=other * PLANE + c))
        copies_z[-1].start()

    to_next.wait()
    to_prev.wait()
    on_next = block(3, y_prev + hi, y_next + hi, 0)
    on_prev = block(4, y_next + hi, y_prev + hi, 1)
    on_next.start()
    on_prev.start()

    for k in range(1, MEMBER_DEV):
        other = (a + k) % MEMBER_DEV
        remote(own_noise, all_noise.at[other], noise_send.at[k], noise_recv.at[other], member=other).wait_recv()
    for k in range(1, MEMBER_DEV):
        other = (a + k) % MEMBER_DEV
        remote(flat_mine, slot(got2, other), s2_send.at[k], s2_recv.at[other], member=other).wait_recv()

    lefts, rights = [], []
    for p in range(PLANES):
        for r in range(3):
            group = ((p * PLANE + c) * 3 + r) % 4
            sig = sigma[pl.ds(group, 1), :]
            wgt = jnp.where(lane1 < 100, 1.0 / (sig * sig), 0.0)
            rec = jnp.concatenate(
                [got2[pl.ds(8 * r + 2 * p + m, 8, stride=24), :] for m in range(2)], 0
            )
            nse = jnp.concatenate([all_noise[:, r, 2 * p + m, :] for m in range(2)], 0)
            innovation = obs[r, p:p + 1, :] + nse - rec
            anomaly = rec - jnp.sum(rec, axis=0, keepdims=True) * (1.0 / 16.0)
            lefts.append(anomaly * wgt)
            rights.append(jnp.concatenate([anomaly, innovation], 0))
    both = lax.dot_general(
        jnp.concatenate(lefts, 1), jnp.concatenate(rights, 1), (((1,), (1,)), ((), ())),
        precision=lax.Precision.HIGHEST, preferred_element_type=jnp.float32,
    )
    gram[:, 0:64] = jnp.concatenate([both[0:8], both[8:16]], 1)
    gram[:, 64:128] = jnp.zeros((8, 64), jnp.float32)

    def exchange(count, me, src, dst, send, recv, tile_of):
        sent = []
        for k in range(1, count):
            other = (me + k) % count
            sent.append(remote(src, dst.at[me], send.at[k], recv.at[me], tile=tile_of(other)))
            sent[-1].start()
        return sent

    def collect(count, me, src, dst, send, recv, tile_of):
        for k in range(1, count):
            other = (me + k) % count
            remote(src, dst.at[other], send.at[k], recv.at[other], tile=tile_of(other)).wait_recv()
        parts = [dst[k] for k in range(count)]
        while len(parts) > 1:
            parts = [parts[i] + parts[i + 1] for i in range(0, len(parts), 2)]
        return parts[0]

    def in_plane(other):
        return z * PLANE + other

    def across(other):
        return other * PLANE + c

    gram1[c] = gram[...]
    sent1 = exchange(PLANE, c, gram, gram1, g1_send, g1_recv, in_plane)

    to_partner.wait()
    par_next = block(5, partner, y_next + hi)
    par_prev = block(6, partner, y_prev + hi)
    par_next.start()
    par_prev.start()

    plane_total = collect(PLANE, c, gram, gram1, g1_send, g1_recv, in_plane)
    gram_plane[...] = plane_total
    gram2[z] = plane_total
    sent2 = exchange(PLANES, z, gram_plane, gram2, g2_send, g2_recv, across)

    total = mine[...]
    for k in range(1, PLANES):
        other = (z + k) % PLANES
        remote(mine, plane_got.at[other], zl_send.at[k], zl_recv.at[other], tile=other * PLANE + c).wait_recv()
        total = total + plane_got[other]
    block_rows[...] = total
    for r in range(3):
        records[:, 100 * r:100 * r + 100] = block_rows[r, pl.ds(2 * z, 2), 0:100]

    par_next.wait()
    par_prev.wait()
    last_next = block(7, y_prev + 1 - hi, y_next + hi, 0)
    last_prev = block(8, y_next + 1 - hi, y_prev + hi, 1)
    last_next.start()
    last_prev.start()

    packed = collect(PLANES, z, gram_plane, gram2, g2_send, g2_recv, across)

    lane16 = lax.broadcasted_iota(jnp.int32, (16, 128), 1)
    row16 = lax.broadcasted_iota(jnp.int32, (16, 128), 0)
    system = jnp.concatenate([packed, pltpu.roll(packed, 96, 1)], 0)
    system = jnp.where(lane16 < 32, system, 0.0) + jnp.where(row16 == lane16, 15.0, 0.0)
    for p in range(16):
        pivot = system[p:p + 1, :] / system[p:p + 1, p:p + 1]
        system = jnp.where(row16 == p, pivot, system - system[:, p:p + 1] * pivot)
    combine = system - jnp.sum(system, axis=0, keepdims=True) * (1.0 / 16.0)
    combine = combine + jnp.where(row16 == lane16 - 16, 1.0, 0.0)
    for m in range(2):
        column = jnp.sum(jnp.where(lane16 == 16 + 8 * m + a, combine, 0.0), axis=1, keepdims=True)
        coef[m] = jnp.broadcast_to(column, (16, 128))

    on_next.wait()
    on_prev.wait()
    last_next.wait()
    last_prev.wait()

    factors = [[jnp.broadcast_to(coef[m, k:k + 1, :], (8, 128)) for k in range(16)] for m in range(2)]
    for r in range(0, 32, 8):
        for i in range(4):
            columns = slice(i * 128, (i + 1) * 128)
            sums = [None, None]
            for k in range(16):
                value = every[k // 2, k % 2, r:r + 8, columns]
                for m in range(2):
                    term = value * factors[m][8 * (k % 2) + k // 2]
                    sums[m] = term if sums[m] is None else sums[m] + term
            for m in range(2):
                updated[m, r:r + 8, columns] = sums[m]

    for copy in noise_copies + copies1 + copies2 + copies_z + sent1 + sent2:
        copy.wait_send()


def shards(surface, depth, land, gauge_cells, sigma, observed, noise):
    f32 = jnp.float32
    groups = jnp.pad(sigma.reshape(4, 100), ((0, 0), (0, 28)), constant_values=1.0)
    hbm = pl.BlockSpec(memory_space=pl.ANY)
    vmem = pl.BlockSpec(memory_space=pltpu.VMEM)
    dma = pltpu.SemaphoreType.DMA
    buffers = [
        (32, 512), None, None, (4, 128), (75, 128), (2, 9600), None, None,
        (ROWS, 8, 128), (ROWS * 4, 128), (ROWS, 8, 128), (ROWS, 8, 128), (ROWS, 8, 128), (ROWS, 8, 128),
        (6 * (OWN + 1) * 32, 128),
        (MEMBER_DEV, 2, 32, 512),
        (24, 8, 128), (PLANE, 3, 8, 128), (3, 8, 128), (MEMBER_DEV * 24, 128),
        (3, 8, 128), (MEMBER_DEV, 3, 8, 128), (3, 8, 128),
        (PLANES, 3, 8, 128), (3, 8, 128),
        (8, 128), (PLANE, 8, 128), (8, 128), (PLANES, 8, 128), (2, 16, 128),
    ]
    scratch = [pltpu.VMEM(shape, f32) if shape else None for shape in buffers]
    scratch[1] = pltpu.VMEM((32, 512), jnp.int32)
    for number in (2, 6, 7):
        scratch[number] = pltpu.SMEM((400,), jnp.int32)
    counts = (15, 4, 4, 8, 8, 8, 8, 8, 8, 4, 4, 8, 8, 4, 4, 9, 9)
    return pl.pallas_call(
        kernel,
        out_shape=(jax.ShapeDtypeStruct((2, 32, 512), f32), jax.ShapeDtypeStruct((2, 300), f32)),
        in_specs=[hbm] * 7,
        out_specs=(vmem, vmem),
        scratch_shapes=scratch + [dma((count,)) for count in counts],
        compiler_params=pltpu.CompilerParams(collective_id=0, has_side_effects=True),
    )(surface, depth, land, gauge_cells, groups, observed.reshape(75, 128), noise)


def solution(mesh):
    in_specs = (
        P("member", "tile", None),
        P("tile", None),
        P("tile", None),
        P(),
        P(),
        P(),
        P("member", None),
    )
    out_specs = (P("member", "tile", None), P("member", "tile"))
    return jax.shard_map(shards, mesh=mesh, in_specs=in_specs, out_specs=out_specs, check_vma=False)
```

```python
import jax
import jax.numpy as jnp
from jax import lax
from jax.experimental import pallas as pl
from jax.experimental.pallas import tpu as pltpu
from jax.sharding import PartitionSpec as P

MESH = pl.DeviceIdType.MESH
HALO = 24
OWN = 32
ROWS = OWN + 2 * HALO
PLANE = 8
PLANES = 4
MEMBER_DEV = 8
NO_GAUGE = OWN * 32


def remote(src, dst, send, recv, **device):
    return pltpu.make_async_remote_copy(
        src_ref=src, dst_ref=dst, send_sem=send, recv_sem=recv, device_id=device, device_id_type=MESH
    )


def next_col(value, lane):
    rolled = pltpu.roll(value, 127, value.ndim - 1)
    return jnp.where(lane == 127, pltpu.roll(rolled, 7, value.ndim - 2), rolled)


def prev_col(value, lane):
    rolled = pltpu.roll(value, 1, value.ndim - 1)
    return jnp.where(lane == 0, pltpu.roll(rolled, 1, value.ndim - 2), rolled)


def merge(low, high, shift, lane):
    both = jnp.where(lane < 128 - shift, pltpu.roll(low, 128 - shift, 1), pltpu.roll(high, 128 - shift, 1))
    return jnp.where(lane < 100, both, 0.0)


def kernel(
    surface, depth, land, cells_in, sigma_in, observed_in, noise_in, updated, records,
    depth_v, land_v, cells, sigma, observed, noise,
    lev, wet, frow, fcol, crow, ccol, hist, every, pieces, got1, mine, got2, own_noise, all_noise, obs,
    plane_got, block_rows, weight, gram, gram1, gram_plane, gram2, coef,
    local_sem, halo_send, halo_recv, noise_send, noise_recv, s1_send, s1_recv, s2_send, s2_recv,
    zl_send, zl_recv, g1_send, g1_recv, g2_send, g2_recv, sur_send, sur_recv,
):
    a = lax.axis_index("member")
    t = lax.axis_index("tile")
    z = t // PLANE
    c = t % PLANE
    y = a // 2
    hi = a % 2
    tiles = PLANE * PLANES
    partner = a + 1 - 2 * hi
    y_next = ((y + 1) % 4) * 2
    y_prev = ((y + 3) % 4) * 2
    above_tile = (t + tiles - 1) % tiles
    below_tile = (t + 1) % tiles

    barrier = pltpu.get_barrier_semaphore()

    def greet(**device):
        pl.semaphore_signal(barrier, inc=1, device_id=device, device_id_type=MESH)

    for k in range(1, MEMBER_DEV):
        greet(member=(a + k) % MEMBER_DEV)
    greet(tile=below_tile)
    greet(tile=above_tile)
    for k in range(1, PLANES):
        greet(tile=((z + k) % PLANES) * PLANE + c)
    for k in range(1, PLANE):
        greet(tile=z * PLANE + (c + k) % PLANE)

    def local(number, src, dst):
        copy = pltpu.make_async_copy(src, dst, local_sem.at[number])
        copy.start()
        return copy

    loads = [local(0, depth, depth_v), local(1, land, land_v)]
    loads += [
        local(
            2 + 4 * m + i,
            surface.at[m, :, pl.ds(i * 128, 128)],
            lev.at[pl.ds(HALO, OWN), 4 * m + i, :],
        )
        for m in range(2)
        for i in range(4)
    ]
    keep = local(10, surface, every.at[a])
    late = [local(11, noise_in, noise), local(12, observed_in, observed), local(13, sigma_in, sigma)]
    table = local(14, cells_in, cells)

    lane = lax.broadcasted_iota(jnp.int32, (8, 128), 1)
    sub = lax.broadcasted_iota(jnp.int32, (8, 128), 0)
    zero = jnp.zeros((8, 128), jnp.float32)
    for r in range(ROWS):
        frow[r] = zero
        fcol[r] = zero
    for s in range(6):
        for p in range(4):
            hist[pl.ds(((s * (OWN + 1) + OWN) * 4 + p) * 8, 8), :] = zero
    loads[0].wait()
    loads[1].wait()
    for r in range(0, OWN, 8):
        for i in range(4):
            columns = slice(i * 128, (i + 1) * 128)
            value = depth_v[r:r + 8, columns] * land_v[r:r + 8, columns].astype(jnp.float32)
            wet[pl.ds((HALO + r) * 4 + i, 8, stride=4), :] = value
    for load in loads[2:]:
        load.wait()
    pl.semaphore_wait(barrier, MEMBER_DEV - 1 + PLANE - 1 + PLANES - 1 + 2)

    halos = [
        remote(lev.at[pl.ds(HALO, HALO)], lev.at[pl.ds(HALO + OWN, HALO)], halo_send.at[0], halo_recv.at[0], tile=above_tile),
        remote(lev.at[pl.ds(OWN, HALO)], lev.at[pl.ds(0, HALO)], halo_send.at[1], halo_recv.at[1], tile=below_tile),
        remote(
            wet.at[pl.ds(HALO * 4, HALO * 4)], wet.at[pl.ds((HALO + OWN) * 4, HALO * 4)],
            halo_send.at[2], halo_recv.at[2], tile=above_tile,
        ),
        remote(
            wet.at[pl.ds(OWN * 4, HALO * 4)], wet.at[pl.ds(0, HALO * 4)],
            halo_send.at[3], halo_recv.at[3], tile=below_tile,
        ),
    ]
    for copy in halos:
        copy.start()

    def block(number, slot, member, part=None):
        ref = every.at[slot] if part is None else every.at[slot, part]
        return remote(ref, ref, sur_send.at[number], sur_recv.at[number], member=member)

    keep.wait()
    to_partner = block(0, a, partner)
    to_next = block(1, a, y_next + hi)
    to_prev = block(2, a, y_prev + hi)
    to_next.start()
    to_prev.start()

    lane1 = lax.broadcasted_iota(jnp.int32, (1, 128), 1)
    lane2 = lax.broadcasted_iota(jnp.int32, (2, 128), 1)
    for load in late:
        load.wait()
    for p in range(PLANES):
        for r in range(3):
            start = ((p * PLANE + c) * 3 + r) * 100
            first, shift = start // 128, start % 128
            after = jnp.minimum(first + 1, 74)
            own_noise[r, 2 * p:2 * p + 2, :] = merge(
                noise[:, pl.ds(pl.multiple_of(first * 128, 128), 128)],
                noise[:, pl.ds(pl.multiple_of(after * 128, 128), 128)],
                shift, lane2,
            )
            obs[r, p:p + 1, :] = merge(observed[pl.ds(first, 1), :], observed[pl.ds(after, 1), :], shift, lane1)
    all_noise[a] = own_noise[...]
    for q in range(4):
        first, shift = 100 * q // 128, 100 * q % 128
        after = min(first + 1, 3)
        sig = merge(sigma[first:first + 1, :], sigma[after:after + 1, :], shift, lane1) if shift else sigma[0:1, :]
        weight[q:q + 1, :] = jnp.where(lane1 < 100, 1.0 / (sig * sig), 0.0)

    edge = (lane == 127) & ((sub & 3) == 3)

    def both_rows(pair):
        value = wet[8 * pair:8 * pair + 8, :]
        other = pltpu.roll(value, 4, 0)
        return [jnp.where(sub < 4, value, other), jnp.where(sub < 4, other, value)]

    def coefficients(first, last):
        below = None
        for pair in range(last // 2 - 1, first // 2 - 1, -1):
            even, odd = both_rows(pair)
            if below is None:
                below = both_rows(last // 2)[0] if last < ROWS else zero
            for r, value, following in ((2 * pair + 1, odd, below), (2 * pair, even, odd)):
                crow[r] = jnp.minimum(value, following)
                ccol[r] = jnp.minimum(value, jnp.where(edge, 0.0, next_col(value, lane)))
            below = even

    coefficients(HALO, HALO + OWN - 2)
    for copy in halos:
        copy.wait()
    to_partner.start()
    noise_copies = []
    for k in range(1, MEMBER_DEV):
        noise_copies.append(
            remote(own_noise, all_noise.at[a], noise_send.at[k], noise_recv.at[a], member=(a + k) % MEMBER_DEV)
        )
        noise_copies[-1].start()
    coefficients(0, HALO)
    coefficients(HALO + OWN - 2, ROWS)

    def advance(first, s):
        low, high = first + 1, ROWS - 1 - first
        level = lev[low - 1:low]
        flux = frow[low - 1:low] - crow[low - 1:low] * (lev[low:low + 1] - level)
        frow[low - 1:low] = flux
        group = (s % 6) * (OWN + 1)
        for start in range(low, high, 16):
            stop = min(start + 16, high)
            lane3 = lax.broadcasted_iota(jnp.int32, (stop - start, 8, 128), 2)
            level = lev[start:stop]
            rows_flux = frow[start:stop] - crow[start:stop] * (lev[start + 1:stop + 1] - level)
            frow[start:stop] = rows_flux
            cols_flux = fcol[start:stop] - ccol[start:stop] * (next_col(level, lane3) - level)
            fcol[start:stop] = cols_flux
            above = jnp.concatenate([flux, rows_flux[:-1]], 0)
            flux = rows_flux[-1:]
            level = level - (rows_flux - above + cols_flux - prev_col(cols_flux, lane3))
            lev[start:stop] = level
            for r in range(max(start, HALO), min(stop, HALO + OWN)):
                flat = ((group + (r - HALO)) * 4 + s // 6) * 8
                hist[pl.ds(pl.multiple_of(flat, 8), 8), :] = level[r - start]

    for first in range(0, 24, 8):
        def one(s, carry, first=first):
            advance(first, s)
            return carry

        lax.fori_loop(first, first + 8, one, 0)

    to_next.wait()
    to_prev.wait()
    on_next = block(3, y_prev + hi, y_next + hi, 0)
    on_prev = block(4, y_next + hi, y_prev + hi, 1)
    on_next.start()
    on_prev.start()

    table.wait()

    def sample(j, totals):
        put = lane == j
        out = []
        for q in range(4):
            cell = cells[q * 100 + j]
            start = ((cell >> 9) & 31) * 32 + ((cell >> 7) & 3)
            start = jnp.where((cell >> 14) == t, start, NO_GAUGE)
            shift = (j - cell) & 127
            for s in range(6):
                found = hist[pl.ds(s * (OWN + 1) * 32 + start, 8, stride=4), :]
                out.append(jnp.where(put, pltpu.roll(found, shift, 1), totals[q * 6 + s]))
        return tuple(out)

    totals = lax.fori_loop(0, 100, sample, (zero,) * 24, unroll=4)
    for q in range(4):
        for s in range(6):
            pieces[4 * s + q] = totals[q * 6 + s]

    copies1 = []
    for k in range(1, PLANE):
        other = (c + k) % PLANE
        copies1.append(
            remote(pieces.at[pl.ds(other * 3, 3)], got1.at[c], s1_send.at[k], s1_recv.at[c], tile=z * PLANE + other)
        )
        copies1[-1].start()
    total = pieces[pl.ds(c * 3, 3)]
    for k in range(1, PLANE):
        other = (c + k) % PLANE
        remote(
            pieces.at[pl.ds(other * 3, 3)], got1.at[other], s1_send.at[k], s1_recv.at[other], tile=z * PLANE + other
        ).wait_recv()
        total = total + got1[other]
    mine[...] = total
    for r in range(3):
        got2[pl.ds(pl.multiple_of(a * 24 + 8 * r, 8), 8), :] = total[r]

    def slot(ref, number):
        return ref.at[pl.ds(pl.multiple_of(number * 24, 8), 24)]

    flat_mine = got2.at[pl.ds(pl.multiple_of(a * 24, 8), 24)]
    copies2 = []
    for k in range(1, MEMBER_DEV):
        other = (a + k) % MEMBER_DEV
        copies2.append(remote(flat_mine, slot(got2, a), s2_send.at[k], s2_recv.at[a], member=other))
        copies2[-1].start()
    copies_z = []
    for k in range(1, PLANES):
        other = (z + k) % PLANES
        copies_z.append(remote(mine, plane_got.at[z], zl_send.at[k], zl_recv.at[z], tile=other * PLANE + c))
        copies_z[-1].start()

    to_partner.wait()
    par_next = block(5, partner, y_next + hi)
    par_prev = block(6, partner, y_prev + hi)
    par_next.start()
    par_prev.start()

    for k in range(1, MEMBER_DEV):
        other = (a + k) % MEMBER_DEV
        remote(own_noise, all_noise.at[other], noise_send.at[k], noise_recv.at[other], member=other).wait_recv()
    for k in range(1, MEMBER_DEV):
        other = (a + k) % MEMBER_DEV
        remote(flat_mine, slot(got2, other), s2_send.at[k], s2_recv.at[other], member=other).wait_recv()

    lefts, rights = [], []
    for p in range(PLANES):
        for r in range(3):
            group = ((p * PLANE + c) * 3 + r) % 4
            wgt = weight[pl.ds(group, 1), :]
            rec = jnp.concatenate(
                [got2[pl.ds(8 * r + 2 * p + m, 8, stride=24), :] for m in range(2)], 0
            )
            nse = jnp.concatenate([all_noise[:, r, 2 * p + m, :] for m in range(2)], 0)
            innovation = obs[r, p:p + 1, :] + nse - rec
            anomaly = rec - jnp.sum(rec, axis=0, keepdims=True) * (1.0 / 16.0)
            lefts.append(anomaly * wgt)
            rights.append(jnp.concatenate([anomaly, innovation], 0))
    both = lax.dot_general(
        jnp.concatenate(lefts, 1), jnp.concatenate(rights, 1), (((1,), (1,)), ((), ())),
        precision=lax.Precision.HIGHEST, preferred_element_type=jnp.float32,
    )
    gram[:, 0:64] = jnp.concatenate([both[0:8], both[8:16]], 1)
    gram[:, 64:128] = jnp.zeros((8, 64), jnp.float32)

    def exchange(count, me, src, dst, send, recv, tile_of):
        sent = []
        for k in range(1, count):
            other = (me + k) % count
            sent.append(remote(src, dst.at[me], send.at[k], recv.at[me], tile=tile_of(other)))
            sent[-1].start()
        return sent

    def collect(count, me, src, dst, send, recv, tile_of):
        for k in range(1, count):
            other = (me + k) % count
            remote(src, dst.at[other], send.at[k], recv.at[other], tile=tile_of(other)).wait_recv()
        parts = [dst[k] for k in range(count)]
        while len(parts) > 1:
            parts = [parts[i] + parts[i + 1] for i in range(0, len(parts), 2)]
        return parts[0]

    def in_plane(other):
        return z * PLANE + other

    def across(other):
        return other * PLANE + c

    gram1[c] = gram[...]
    sent1 = exchange(PLANE, c, gram, gram1, g1_send, g1_recv, in_plane)

    par_next.wait()
    par_prev.wait()
    last_next = block(7, y_prev + 1 - hi, y_next + hi, 0)
    last_prev = block(8, y_next + 1 - hi, y_prev + hi, 1)
    last_next.start()
    last_prev.start()

    plane_total = collect(PLANE, c, gram, gram1, g1_send, g1_recv, in_plane)
    gram_plane[...] = plane_total
    gram2[z] = plane_total
    sent2 = exchange(PLANES, z, gram_plane, gram2, g2_send, g2_recv, across)

    total = mine[...]
    for k in range(1, PLANES):
        other = (z + k) % PLANES
        remote(mine, plane_got.at[other], zl_send.at[k], zl_recv.at[other], tile=other * PLANE + c).wait_recv()
        total = total + plane_got[other]
    block_rows[...] = total
    for r in range(3):
        records[:, 100 * r:100 * r + 100] = block_rows[r, pl.ds(2 * z, 2), 0:100]

    packed = collect(PLANES, z, gram_plane, gram2, g2_send, g2_recv, across)

    lane16 = lax.broadcasted_iota(jnp.int32, (16, 128), 1)
    row16 = lax.broadcasted_iota(jnp.int32, (16, 128), 0)
    system = jnp.concatenate([packed, pltpu.roll(packed, 96, 1)], 0)
    system = jnp.where(lane16 < 32, system, 0.0) + jnp.where(row16 == lane16, 15.0, 0.0)
    for p in range(16):
        pivot = system[p:p + 1, :] / system[p:p + 1, p:p + 1]
        system = jnp.where(row16 == p, pivot, system - system[:, p:p + 1] * pivot)
    combine = system - jnp.sum(system, axis=0, keepdims=True) * (1.0 / 16.0)
    combine = combine + jnp.where(row16 == lane16 - 16, 1.0, 0.0)
    for m in range(2):
        column = jnp.sum(jnp.where(lane16 == 16 + 8 * m + a, combine, 0.0), axis=1, keepdims=True)
        coef[m] = jnp.broadcast_to(column, (16, 128))

    on_next.wait()
    on_prev.wait()
    last_next.wait()
    last_prev.wait()

    factors = [[jnp.broadcast_to(coef[m, k:k + 1, :], (8, 128)) for k in range(16)] for m in range(2)]
    for r in range(0, 32, 8):
        for i in range(4):
            columns = slice(i * 128, (i + 1) * 128)
            sums = [None, None]
            for k in range(16):
                value = every[k // 2, k % 2, r:r + 8, columns]
                for m in range(2):
                    term = value * factors[m][8 * (k % 2) + k // 2]
                    sums[m] = term if sums[m] is None else sums[m] + term
            for m in range(2):
                updated[m, r:r + 8, columns] = sums[m]

    for copy in noise_copies + copies1 + copies2 + copies_z + sent1 + sent2:
        copy.wait_send()


def shards(surface, depth, land, gauge_cells, sigma, observed, noise):
    f32 = jnp.float32
    groups = jnp.pad(sigma, (0, 112), constant_values=1.0).reshape(4, 128)
    hbm = pl.BlockSpec(memory_space=pl.ANY)
    vmem = pl.BlockSpec(memory_space=pltpu.VMEM)
    dma = pltpu.SemaphoreType.DMA
    buffers = [
        (32, 512), None, None, (4, 128), (75, 128), (2, 9600),
        (ROWS, 8, 128), (ROWS * 4, 128), (ROWS, 8, 128), (ROWS, 8, 128), (ROWS, 8, 128), (ROWS, 8, 128),
        (6 * (OWN + 1) * 32, 128),
        (MEMBER_DEV, 2, 32, 512),
        (24, 8, 128), (PLANE, 3, 8, 128), (3, 8, 128), (MEMBER_DEV * 24, 128),
        (3, 8, 128), (MEMBER_DEV, 3, 8, 128), (3, 8, 128),
        (PLANES, 3, 8, 128), (3, 8, 128), (8, 128),
        (8, 128), (PLANE, 8, 128), (8, 128), (PLANES, 8, 128), (2, 16, 128),
    ]
    scratch = [pltpu.VMEM(shape, f32) if shape else None for shape in buffers]
    scratch[1] = pltpu.VMEM((32, 512), jnp.int32)
    scratch[2] = pltpu.SMEM((400,), jnp.int32)
    counts = (15, 4, 4, 8, 8, 8, 8, 8, 8, 4, 4, 8, 8, 4, 4, 9, 9)
    return pl.pallas_call(
        kernel,
        out_shape=(jax.ShapeDtypeStruct((2, 32, 512), f32), jax.ShapeDtypeStruct((2, 300), f32)),
        in_specs=[hbm] * 7,
        out_specs=(vmem, vmem),
        scratch_shapes=scratch + [dma((count,)) for count in counts],
        compiler_params=pltpu.CompilerParams(collective_id=0, has_side_effects=True),
    )(surface, depth, land, gauge_cells, groups, observed.reshape(75, 128), noise)


def solution(mesh):
    in_specs = (
        P("member", "tile", None),
        P("tile", None),
        P("tile", None),
        P(),
        P(),
        P(),
        P("member", None),
    )
    out_specs = (P("member", "tile", None), P("member", "tile"))
    return jax.shard_map(shards, mesh=mesh, in_specs=in_specs, out_specs=out_specs, check_vma=False)
```
